32 devices in a mesh: band: 4 (over y, x), slab: 8 (over z, core).
Axes of the slice: x: 2, y: 2, z: 4, core: 2. Of those that a mesh axis runs over, the one named last changes fastest.
Arguments:
- coefficients: float32 [8, 96, 96, 192], P('band', 'slab'), may hold values from -6 to 6
- occupation: int32 [8], P('band'), may hold values from 1 to 2
- pencil_reach: int32 [96, 96], P('slab'), may hold values from -1 to 47
- external: float32 [192, 192, 192], P(None, 'slab'), may hold values from -3 to 3
Outputs:
- applied: float32 [8, 96, 96, 192], P('band', 'slab')
- potential: float32 [192, 192, 192], P(None, 'slab')
The draws below stay inside these ranges and needn't reach their ends.
All inputs are finite; a program needn't handle non-finite values.
Results may differ from the reference program's by a relative error of at most 0.00011.
Values sent between devices are 32-bit elements; how exact they have to be, the bound alone decides.
A program may use at most 128 MiB of HBM per device.

```python
import jax
import jax.numpy as jnp
from jax import lax

NW = 96
NG = 192
BANDS = 8


def draw_pencil_reach(key, part):
    halfway = NW // 2
    key_radius = jax.random.fold_in(key, 11)
    key_jitter = jax.random.fold_in(key, 23)
    radius_sq = jax.random.randint(key_radius, (), (halfway - 1) * (halfway - 1), halfway * halfway, dtype=jnp.int32)
    indices = jnp.arange(NW, dtype=jnp.int32)
    frequencies = jnp.where(indices < halfway, indices, indices - NW)
    planar = frequencies[:, None] * frequencies[:, None] + frequencies[None, :] * frequencies[None, :]
    offsets = jnp.arange(halfway + 1, dtype=jnp.int32)
    inside = planar[:, :, None] + offsets[None, None, :] * offsets[None, None, :] <= radius_sq
    extent = jnp.sum(inside.astype(jnp.int32), axis=2) - 1
    jitter = jax.random.randint(key_jitter, (NW, NW), 0, 2, dtype=jnp.int32)
    jitter = jnp.where(planar == 0, 0, jitter)
    return jnp.maximum(extent - jitter, -1)


def place_ends(values, key, smallest, largest):
    shape = values.shape
    index_at = [jax.random.randint(jax.random.fold_in(key, axis), (), 0, shape[axis]) for axis in range(len(shape))]
    values = values.at[tuple(index_at)].set(smallest)
    longest = shape.index(max(shape))
    index_at[longest] = (index_at[longest] + 1) % shape[longest]
    return values.at[tuple(index_at)].set(largest)


def block_levels(rng, dims, shards, least, high):
    level, own = 1.0, jax.random.fold_in(rng, 6)
    for dim, shards_of in shards:
        heights = jnp.exp(jax.random.uniform(jax.random.fold_in(own, dim), (shards_of,), jnp.float32, least / len(shards), high / len(shards)))
        level = level * jnp.repeat(heights, dims[dim] // shards_of).reshape([-1 if axis == dim else 1 for axis in range(len(dims))])
    return level


def centred(key, shape, deviation, most, shards=(), kind=jnp.bfloat16):
    result = jax.random.normal(key, shape, jnp.float32) * deviation
    if len(shards) > 0:
        result = block_levels(key, shape, shards, -0.22, 0.18) * result
    return jnp.clip(result, min=-most, max=most).astype(kind)


def setup_inputs(seed: int = 0) -> dict:
    keys = jax.random.split(jax.random.key(seed), 5)
    coefficients = centred(keys[0], (BANDS, NW, NW, 2 * NW), 1.0, 6.0, ((0, 4), (1, 8)), jnp.float32)
    occupation = place_ends(jax.random.randint(keys[1], (BANDS,), 1, 3), jax.random.fold_in(keys[1], 1), 1, 2).astype(jnp.int32)
    pencil_reach = draw_pencil_reach(jax.random.fold_in(keys[4], 71), 0)
    external = centred(keys[3], (NG, NG, NG), 0.5, 3.0, ((1, 8),), jnp.float32)
    return dict(coefficients=coefficients, occupation=occupation, pencil_reach=pencil_reach, external=external)


KINETIC = 0.0005
SLATER = 0.9847


def frequency(length):
    indices = jnp.arange(length, dtype=jnp.int32)
    return jnp.where(indices < length // 2, indices, indices - length)


def embed_grid(values):
    halfway = NW // 2
    for dimension in range(3):
        lower = lax.slice_in_dim(values, 0, halfway, axis=dimension)
        upper = lax.slice_in_dim(values, halfway, NW, axis=dimension)
        padding_shape = list(values.shape)
        padding_shape[dimension] = NG - NW
        values = jnp.concatenate([lower, jnp.zeros(padding_shape, values.dtype), upper], axis=dimension)
    return values


def extract_grid(values):
    halfway = NW // 2
    for dimension in range(3):
        lower = lax.slice_in_dim(values, 0, halfway, axis=dimension)
        upper = lax.slice_in_dim(values, NG - halfway, NG, axis=dimension)
        values = jnp.concatenate([lower, upper], axis=dimension)
    return values


def to_real(coefficient, sphere):
    real_part = coefficient[..., :NW] * sphere
    imag_part = coefficient[..., NW:] * sphere
    spectrum = lax.complex(real_part, imag_part)
    return jnp.fft.ifftn(embed_grid(spectrum)) * (NG ** 3 / NW ** 1.5)


def reference(coefficients, occupation, pencil_reach, external):
    wavenumbers = frequency(NW)
    sphere = (jnp.abs(wavenumbers)[None, None, :] <= pencil_reach[:, :, None]).astype(jnp.float32)
    weights = occupation.astype(jnp.float32) / BANDS

    def add_band(running, members):
        coefficient, weight = members
        wavefield = to_real(coefficient, sphere)
        squares = jnp.real(wavefield) * jnp.real(wavefield) + jnp.imag(wavefield) * jnp.imag(wavefield)
        return running + weight * squares, None

    density, _ = lax.scan(add_band, jnp.zeros((NG, NG, NG), jnp.float32), (coefficients, weights))
    potential_xyz = jnp.transpose(external, (0, 2, 1)) - SLATER * jnp.cbrt(density)
    squared = (wavenumbers * wavenumbers).astype(jnp.float32)
    kinetic = KINETIC * (squared[:, None, None] + squared[None, :, None] + squared[None, None, :])

    def apply_band(coefficient):
        wavefield = to_real(coefficient, sphere)
        returned = extract_grid(jnp.fft.fftn(wavefield * potential_xyz)) * (NW ** 1.5 / NG ** 3)
        real_out = sphere * (kinetic * (coefficient[..., :NW] * sphere) + jnp.real(returned))
        imag_out = sphere * (kinetic * (coefficient[..., NW:] * sphere) + jnp.imag(returned))
        return jnp.concatenate([real_out, imag_out], axis=-1)

    applied = lax.map(apply_band, coefficients)
    return applied, jnp.transpose(potential_xyz, (0, 2, 1))
```

```python
import math

import jax
import jax.numpy as jnp
import numpy as np
from jax import lax
from jax.sharding import PartitionSpec as P

KINETIC = 0.0005
SLATER = 0.9847
PARTS = 3


def frequency(length):
    indices = jnp.arange(length, dtype=jnp.int32)
    return jnp.where(indices < length // 2, indices, indices - length)


def inverse_table(length, extent):
    wavenumbers = frequency(length)
    positions = jnp.arange(extent, dtype=jnp.int32)
    phases = positions[:, None] * wavenumbers[None, :] % extent
    angles = phases.astype(jnp.float32) * (2.0 * math.pi / extent)
    factor = length ** (-0.5)
    cosine = jnp.cos(angles) * factor
    sine_part = jnp.sin(angles) * factor
    return jnp.stack([jnp.stack([cosine, -sine_part], 1), jnp.stack([sine_part, cosine], 1)], 0)


def forward_table(length, extent):
    wavenumbers = frequency(length)
    positions = jnp.arange(extent, dtype=jnp.int32)
    phases = wavenumbers[:, None] * positions[None, :] % extent
    angles = phases.astype(jnp.float32) * (2.0 * math.pi / extent)
    factor = length**0.5 / extent
    cosine = jnp.cos(angles) * factor
    sine_part = jnp.sin(angles) * factor
    return jnp.stack([jnp.stack([cosine, sine_part], 1), jnp.stack([-sine_part, cosine], 1)], 0)


def contract(form, left, right):
    return jnp.einsum(form, left, right, precision=lax.Precision.HIGH)


def slab_plan(coefficients, occupation, pencil_reach, external):
    nbands, planes, width, doubled = coefficients.shape
    points = 2 * width
    slabs = lax.axis_size("slab")
    layers = points // slabs
    groups = lax.axis_size("band")
    inverse = inverse_table(width, points)
    forward = forward_table(width, points)
    wavenumbers = frequency(width)
    sphere = (jnp.abs(wavenumbers)[None, None, :] <= pencil_reach[:, :, None]).astype(jnp.float32)
    sphere_full = sphere[None, :, :, None, :]
    masked = coefficients.reshape(nbands, planes, width, 2, width) * sphere_full
    along_z = contract("bxgci,onci->bxnog", masked, inverse)
    flattened = along_z.reshape(nbands, planes, points, 2 * width)
    received = lax.all_to_all(flattened, "slab", split_axis=2, concat_axis=1, tiled=True)
    columns = received.reshape(received.shape[0], width, layers, 2, width)
    spread = contract("bkzcg,oycg->bkzoy", columns, inverse)
    wavefield = contract("bkzcy,oxck->bxzoy", spread, inverse)
    squares = jnp.sum(wavefield * wavefield, axis=3)
    weights = occupation.astype(jnp.float32) / (nbands * groups)
    partial_value = contract("b,bxzy->xzy", weights, squares)
    rows_all = points * layers
    share = (rows_all + groups - 1) // groups
    flat_partial = partial_value.reshape(rows_all, points)
    density = lax.psum_scatter(flat_partial, "band", scatter_dimension=0, tiled=True)
    flat_external = external.reshape(rows_all, points)
    start_row = lax.axis_index("band") * share
    own_external = lax.dynamic_slice_in_dim(flat_external, start_row, share, 0)
    own_potential = own_external - SLATER * jnp.cbrt(density)
    gathered = lax.all_gather(own_potential, "band", axis=0, tiled=True)
    potential_all = gathered.reshape(points, layers, points)
    product = wavefield * potential_all[None, :, :, None, :]
    back_rows = contract("bxzcy,okcx->bkzoy", product, forward)
    back_y = contract("bkzcy,ogcy->bkzog", back_rows, forward).reshape(
        nbands, width, layers, 2 * width
    )
    received = lax.all_to_all(back_y, "slab", split_axis=1, concat_axis=2, tiled=True)
    blocks = received.reshape(received.shape[0], planes, points, 2, width)
    returned = contract("bxncg,ohcn->bxgoh", blocks, forward)
    plane_index = lax.axis_index("slab") * planes + jnp.arange(planes, dtype=jnp.int32)
    plane_freq = jnp.where(plane_index < width // 2, plane_index, plane_index - width)
    plane_sq = (plane_freq * plane_freq).astype(jnp.float32)
    wave_sq = (wavenumbers * wavenumbers).astype(jnp.float32)
    kinetic = KINETIC * (plane_sq[:, None, None] + wave_sq[None, :, None] + wave_sq[None, None, :])
    finished = sphere_full * (kinetic[None, :, :, None, :] * masked + returned)
    return (finished.reshape(nbands, planes, width, 2 * width), potential_all)


def tables(length, extent):
    indices = np.arange(length)
    wavenumbers = np.where(indices < length // 2, indices, indices - length)
    angles = (np.arange(extent)[:, None] * wavenumbers[None, :] % extent) * (2.0 * math.pi / extent)
    cosine, sine = np.cos(angles), np.sin(angles)
    inverse = np.stack([np.stack([cosine, -sine], 1), np.stack([sine, cosine], 1)], 0) * length ** -0.5
    cosine, sine = cosine.T, sine.T
    forward = np.stack([np.stack([cosine, sine], 1), np.stack([-sine, cosine], 1)], 0) * (length**0.5 / extent)
    return inverse.astype(np.float32), forward.astype(np.float32)


def exchange_plan(coefficients, occupation, pencil_reach, external, parts):
    nbands, planes, width, doubled = coefficients.shape
    points = 2 * width
    slabs = lax.axis_size("slab")
    groups = lax.axis_size("band")
    layers = points // slabs
    own = layers // groups
    count = own // parts
    everyone = ("band", "slab")
    members = groups * slabs
    group = lax.axis_index("band")
    inverse, forward = tables(width, points)
    wavenumbers = frequency(width)
    sphere = (jnp.abs(wavenumbers)[None, None, :] <= pencil_reach[:, :, None]).astype(jnp.float32)
    sphere_full = jnp.concatenate([sphere, sphere], 2)[None]
    masked = coefficients * sphere_full
    rows = masked.reshape(nbands * planes * width, doubled)

    inverse_z = inverse.reshape(2, slabs, groups, parts, count, 2, width).transpose(3, 2, 1, 4, 0, 5, 6)
    inverse_z = inverse_z.reshape(parts, members * count * 2, doubled)
    forward_z = forward.reshape(2, width, 2, slabs, groups, parts, count).transpose(5, 4, 3, 6, 2, 0, 1)
    forward_z = forward_z.reshape(parts, members * count * 2, doubled)

    def swaps(shift):
        if groups & (groups - 1) == 0:
            return [(source, source ^ shift) for source in range(groups)], group ^ shift
        return [(source, (source + shift) % groups) for source in range(groups)], (group - shift) % groups

    def around(value):
        found = {0: value}
        for shift in range(1, groups):
            found[shift] = lax.ppermute(value, "band", swaps(shift)[0])
        origins = {shift: swaps(shift)[1] for shift in found}
        whole = []
        for member in range(groups):
            chosen = value
            for shift in range(1, groups):
                chosen = jnp.where(origins[shift] == member, found[shift], chosen)
            whole.append(chosen)
        return jnp.stack(whole)

    weights = around(occupation.astype(jnp.float32) / (nbands * groups)).reshape(-1)
    own_external = lax.dynamic_slice_in_dim(external, group * own, own, 1)

    def spread_out(along_z):
        return lax.all_to_all(along_z.reshape(members, count * 2, rows.shape[0]), everyone, 0, 0, tiled=True)

    def transform(part, current):
        current = current.reshape(groups, slabs, count, 2, nbands, planes, width)
        spread = contract("gszcbkw,oycw->zgbskoy", current, inverse)
        spread = spread.reshape(count, groups * nbands, slabs * planes, 2, points)
        wavefield = contract("zbkcy,oxck->zboxy", spread, inverse)
        density = jnp.sum(weights[None, :, None, None] * jnp.sum(wavefield * wavefield, 2), 1)
        potential = own_external[:, part * count:(part + 1) * count].transpose(1, 0, 2) - SLATER * jnp.cbrt(density)
        product = wavefield * potential[:, None, None]
        back_x = contract("zbcxy,okcx->zbkoy", product, forward)
        back_y = contract("zbkcy,owcy->zbkow", back_x, forward)
        back_y = back_y.reshape(count, groups, nbands, slabs, planes, 2, width).transpose(1, 3, 0, 5, 2, 4, 6)
        return back_y.reshape(members, count * 2, rows.shape[0]), potential

    def gather_back(block):
        return lax.all_to_all(block, everyone, 0, 0, tiled=True)

    def finish(part, block):
        return contract("rn,rk->nk", block.reshape(members * count * 2, rows.shape[0]), forward_z[part])

    def after(value, *earlier):
        corner = (0,) * value.ndim
        marks = [(other[(0,) * other.ndim] > 3e38).astype(value.dtype) for other in earlier]
        return value.at[corner].add(sum(marks))

    worked = []
    arriving = spread_out(contract("rk,nk->rn", inverse_z[0], rows))
    for part in range(parts):
        arrived = arriving
        if part + 1 < parts:
            outgoing = contract("rk,nk->rn", inverse_z[part + 1], rows)
            arriving = spread_out(after(outgoing, worked[-1][0]) if worked else outgoing)
        worked.append(transform(part, arrived))
    returned = 0.0
    for part in range(parts):
        block = worked[part][0]
        if part + 2 < parts:
            block = after(block, worked[part + 1][0])
        returned = returned + finish(part, gather_back(block))
    own_potential = jnp.concatenate([potential for _, potential in worked], 0)
    gathered = lax.all_gather(own_potential, "band", axis=0, tiled=True)
    potential_all = gathered.transpose(1, 0, 2)
    plane_index = lax.axis_index("slab") * planes + jnp.arange(planes, dtype=jnp.int32)
    plane_freq = jnp.where(plane_index < width // 2, plane_index, plane_index - width)
    plane_sq = (plane_freq * plane_freq).astype(jnp.float32)
    wave_sq = (wavenumbers * wavenumbers).astype(jnp.float32)
    twice_sq = jnp.concatenate([wave_sq, wave_sq])
    kinetic = KINETIC * (plane_sq[:, None, None] + wave_sq[None, :, None] + twice_sq[None, None, :])
    finished = sphere_full * (kinetic[None] * masked + returned.reshape(masked.shape))
    return (finished, potential_all)


def shards(*operands):
    layers = 2 * operands[0].shape[2] // lax.axis_size("slab")
    groups = lax.axis_size("band")
    if layers % groups == 0:
        own = layers // groups
        parts = next(p for p in (PARTS, 2, 3, 1) if own % p == 0)
        return exchange_plan(*operands, parts)
    return slab_plan(*operands)


def solution(mesh):
    return jax.shard_map(
        shards,
        mesh=mesh,
        in_specs=(P("band", "slab", None, None), P("band"), P("slab", None), P(None, "slab", None)),
        out_specs=(P("band", "slab", None, None), P(None, "slab", None)),
        check_vma=False,
    )
```
